32 devices in a mesh: row: 4 (over x, core), col: 8 (over z, y).
Axes of the slice: x: 2, y: 2, z: 4, core: 2. Of those that a mesh axis runs over, the one named last changes fastest.
Arguments:
- kernel: bfloat16 [32768, 32768], P('row', 'col'), may hold values from -1 to 1
- random_cols: bfloat16 [32768, 256], P('row'), may hold values from -6 to 6
- tree_perm: int32 [32768], replicated, may hold values from 0 to 32767, as said below
- leaf_units: int32 [32], replicated, may hold values from 1 to 8, 160 in all
Outputs:
- bases: bfloat16 [4, 32768, 256], P(None, ('row', 'col'))
The draws below stay inside these ranges and needn't reach their ends.
Inputs may be any that keep to these rules, and one draw needn't show every extreme that they name: `tree_perm`: A permutation. Cut tree positions and stored rows alike into blocks of 1024 in order: every tree block takes at most 32 rows from any one stored block, some pair of blocks shares exactly 32, and every stored block gives 1024 rows in all. `leaf_units`: they sum to 160.
All inputs are finite; a program needn't handle non-finite values.
Results may differ from the reference program's by a relative error of at most 0.0067.
Values may be sent and summed in bfloat16 or wider, within the bound.
A program may use at most 192 MiB of HBM per device.

```python
import math
import jax
import jax.numpy as jnp
import numpy as np
from jax import lax

N = 32768
S = 256
UNIT = 128
MINU = 4
MOSTU = 8
LEAVES = 32
LEVELS = 3
ROWS_DEV = 1024


def draw_kernel(key, part):
    point_key, noise_key, weight_key = jax.random.split(key, 3)
    spread_width = 0.08
    amplitude = 0.5
    points = jax.random.uniform(point_key, (N, 3), jnp.float32)
    norms = jnp.sum(points * points, axis=1)
    block = min(N, 512)
    groups = N // ROWS_DEV
    spacing = jax.random.permutation(weight_key, groups).astype(jnp.float32) / max(groups - 1, 1)
    group_weight = jnp.exp(jnp.log(10.0) * spacing)
    row_weight = jnp.repeat(group_weight, ROWS_DEV, total_repeat_length=N)

    def one_block(index):
        chosen = lax.dynamic_slice_in_dim(points, index * block, block, 0)
        chosen_norms = lax.dynamic_slice_in_dim(norms, index * block, block, 0)
        chosen_weight = lax.dynamic_slice_in_dim(row_weight, index * block, block, 0)
        cross = jnp.dot(chosen, points.T, precision=lax.Precision.HIGHEST)
        distance = jnp.maximum(chosen_norms[:, None] + norms[None, :] - 2.0 * cross, 0.0)
        noise = jax.random.truncated_normal(jax.random.fold_in(noise_key, index), -4.0, 4.0, (block, N), jnp.float32)
        entries = (jnp.exp(-distance / (2.0 * spread_width * spread_width)) + amplitude * noise) * N ** (-0.5)
        return (entries * chosen_weight[:, None]).astype(jnp.bfloat16)
    blocks = lax.map(one_block, jnp.arange(N // block, dtype=jnp.int32))
    return blocks.reshape(N, N)


def random_rows(key, count, length):
    scores = jax.random.randint(key, (count, length), 0, 2 ** 20) * length + jnp.arange(length, dtype=jnp.int32)[None, :]
    return jnp.argsort(scores, axis=1).astype(jnp.int32)


def draw_tree_perm(key, part):
    devices = N // ROWS_DEV
    first_key, second_key, third_key = jax.random.split(jax.random.fold_in(key, 17), 3)
    device_order = jax.random.permutation(first_key, devices).astype(jnp.int32)
    within = random_rows(second_key, devices, ROWS_DEV)
    base = (jnp.arange(devices, dtype=jnp.int32) * ROWS_DEV)[:, None]
    source = jnp.take(device_order, (within + base) % devices).reshape(-1)
    grouped = jnp.argsort(source * N + jnp.arange(N, dtype=jnp.int32)).astype(jnp.int32)
    ranks = random_rows(third_key, devices, ROWS_DEV)
    stored = (base + ranks).reshape(-1)
    return jnp.zeros((N,), jnp.int32).at[grouped].set(stored)


def levels(stream_key, dims, cuts, smallest, largest):
    level = 1.0
    for position, blocks in cuts:
        steps = jax.random.uniform(jax.random.fold_in(jax.random.fold_in(stream_key, 6), position), (blocks,), jnp.float32, smallest / len(cuts), largest / len(cuts))
        level = level * jnp.repeat(jnp.exp(steps), dims[position] // blocks).reshape((-1,) + (1,) * (len(dims) - 1 - position))
    return level


def profile(count, total, bound, lean):
    loads = [(1 << 20) // math.isqrt(standing ** lean) + 1 for standing in range(2, count + 1)]
    surplus, counts = total - bound - (count - 1), [1] * (count - 1)
    while surplus > 0:
        candidates = [i for i in range(count - 1) if counts[i] < bound]
        whole, left = sum([loads[i] for i in candidates]), surplus
        for i in candidates:
            extra = min(bound - counts[i], max(1, left * loads[i] // whole), surplus)
            counts[i] = counts[i] + extra
            surplus = surplus - extra
    return np.array([bound] + counts)


def uneven(rng, number_of, total, most, skew):
    if number_of == 2:
        one = jax.random.randint(rng, (), max(1, total - most), min(most, total - 1) + 1)
        return jnp.stack([one, total - one])
    lengths = jnp.asarray(profile(number_of, total, most, skew), jnp.int32)
    twos = (number_of - 1) // 2
    giver, taker = lengths[1:1 + 2 * twos:2], lengths[2:2 + 2 * twos:2]
    room = jnp.minimum(giver - 1, most - taker)
    moved = jax.random.randint(jax.random.fold_in(rng, 1), (twos,), 0, 1 << 20) % (room + 1)
    lengths = lengths.at[1:1 + 2 * twos:2].set(giver - moved).at[2:2 + 2 * twos:2].set(taker + moved)
    return lengths[jax.random.permutation(jax.random.fold_in(rng, 2), number_of)]


def centred(rng, shape, deviation, reach, cuts=(), kind=jnp.bfloat16):
    factor_of = levels(rng, shape, cuts, -0.22, 0.18) if cuts else 1.0
    drawn = jax.random.normal(rng, shape, jnp.float32) * deviation * factor_of
    return jnp.minimum(jnp.maximum(drawn, -reach), reach).astype(kind)


def setup_inputs(seed: int = 0) -> dict:
    key_list = jax.random.split(jax.random.key(seed), 5)
    return {
        "kernel": draw_kernel(jax.random.fold_in(key_list[4], 71), 0),
        "random_cols": centred(key_list[1], (N, S), 1.0, 6.0, ((0, 4),)),
        "tree_perm": draw_tree_perm(jax.random.fold_in(key_list[4], 71), 0),
        "leaf_units": uneven(key_list[3], LEAVES, N // UNIT - (MINU - 1) * LEAVES, MOSTU, 1).astype(jnp.int32),
    }


def reference(kernel, random_cols, tree_perm, leaf_units):
    partial_w = lax.dot_general(kernel.astype(jnp.float32), random_cols.astype(jnp.float32), (((0,), (0,)), ((), ())), preferred_element_type=jnp.float32)
    sample_w = partial_w.astype(jnp.bfloat16)
    sample = jnp.dot(kernel.astype(jnp.float32), sample_w.astype(jnp.float32), preferred_element_type=jnp.float32).astype(jnp.bfloat16)
    tree_rows = jnp.take(sample, tree_perm.astype(jnp.int32), axis=0)
    sizes = (UNIT * (MINU - 1 + leaf_units)).astype(jnp.int32)
    ends = jnp.cumsum(sizes).astype(jnp.int32)
    positions = jnp.arange(N, dtype=jnp.int32)
    leaf_of = jnp.sum(positions[:, None] >= ends[None, :], axis=1).astype(jnp.int32)

    def leaf_gram(leaf):
        masked = jnp.where((leaf_of == leaf)[:, None], tree_rows, jnp.zeros((), jnp.bfloat16))
        return jnp.dot(masked.T.astype(jnp.float32), tree_rows.astype(jnp.float32), preferred_element_type=jnp.float32)
    leaf_grams = lax.map(leaf_gram, jnp.arange(LEAVES, dtype=jnp.int32))
    values = tree_rows.astype(jnp.float32)
    results = []
    for level in range(LEVELS + 1):
        group = 2 ** level
        count = LEAVES // group
        node_grams = leaf_grams.reshape(count, group, S, S).sum(axis=1)
        node_sizes = sizes.reshape(count, group).sum(axis=1).astype(jnp.float32)
        factor = jnp.linalg.cholesky(node_grams / node_sizes[:, None, None])
        node_of = leaf_of // group

        def add_node(total, node):
            solved = jax.scipy.linalg.solve_triangular(factor[node], values.T, lower=True).T
            return (total + jnp.where((node_of == node)[:, None], solved, jnp.zeros((), jnp.float32)), None)
        total, unused = lax.scan(add_node, jnp.zeros((N, S), jnp.float32), jnp.arange(count, dtype=jnp.int32))
        results.append(total.astype(jnp.bfloat16))
    return jnp.stack(results)
```

```python
import jax
import jax.numpy as jnp
from jax import lax
from jax.experimental import pallas as pl
from jax.experimental.pallas import tpu as pltpu
from jax.sharding import PartitionSpec as P

UNIT = 128
MINU = 4
MOSTU = 8
LEVELS = 3
BLOCK = 64
HIGHEST = lax.Precision.HIGHEST


def basis_kernel(index_ref, gram_ref, rows_ref, out_ref, work, block, high, low):
    nodes, _, half = gram_ref.shape
    width = 2 * half
    count = width // BLOCK
    eye = (
        lax.broadcasted_iota(jnp.int32, (width, width), 0)
        == lax.broadcasted_iota(jnp.int32, (width, width), 1)
    ).astype(jnp.float32)

    @pl.loop(0, nodes)
    def _(node):
        work[node, :half, :half] = gram_ref[node, :half, :]
        work[node, :half, half:width] = gram_ref[node, half:width, :]
        work[node, half:, :half] = jnp.zeros((half, half), jnp.float32)
        work[node, half:, half:width] = gram_ref[node, width:, :]
        work[node, :, width:] = eye

    small = (
        lax.broadcasted_iota(jnp.int32, (nodes, BLOCK, BLOCK), 1)
        == lax.broadcasted_iota(jnp.int32, (nodes, BLOCK, BLOCK), 2)
    )

    @pl.loop(0, count)
    def _(step):
        for which in range(count):

            @pl.when(step == which)
            def _():
                start = which * BLOCK
                block[:, :, :BLOCK] = work[:, start : start + BLOCK, start : start + BLOCK]
                block[:, :, BLOCK:] = small.astype(jnp.float32)

        for column in range(BLOCK - 1):
            base = column // 8 * 8
            rest = block[:, base:, :]
            pivot_row = rest[:, column - base : column - base + 1, :]
            scale = 1.0 / pivot_row[:, :, column : column + 1]
            below = (
                lax.broadcasted_iota(jnp.int32, (nodes, BLOCK - base, 1), 1) > column - base
            )
            factor = jnp.where(below, rest[:, :, column : column + 1], 0.0)
            block[:, base:, :] = rest - factor * (pivot_row * scale)
        pivots = jnp.sum(jnp.where(small, block[:, :, :BLOCK], 0.0), axis=2, keepdims=True)
        block[:, :, BLOCK:] = block[:, :, BLOCK:] * lax.rsqrt(pivots)

        for which in range(count):

            @pl.when(step == which)
            def _():
                start = which * BLOCK
                after = start + BLOCK
                left = start // 128 * 128
                right = width + (after + 127) // 128 * 128

                @pl.loop(0, nodes)
                def _(node):
                    inverse = block[node][:, BLOCK:]
                    solved = jnp.dot(
                        inverse,
                        work[node, start:after, left:right],
                        preferred_element_type=jnp.float32,
                        precision=HIGHEST,
                    )
                    work[node, start:after, left:right] = solved
                    if after < width:
                        panel = solved[:, : width - left].T
                        change = jnp.dot(
                            panel[after - left :, :],
                            solved,
                            preferred_element_type=jnp.float32,
                            precision=HIGHEST,
                        )
                        work[node, after:, left:right] = work[node, after:, left:right] - change

    @pl.loop(0, nodes)
    def _(node):
        full = work[node, :, width:]
        top = full.astype(jnp.bfloat16)
        high[node] = top
        low[node] = (full - top.astype(jnp.float32)).astype(jnp.bfloat16)

    levels, rows, _ = out_ref.shape
    units = rows // UNIT

    @pl.loop(0, levels)
    def _(level):
        @pl.loop(0, units)
        def _(unit):
            node = index_ref[level * units + unit]
            where = pl.ds(pl.multiple_of(unit * UNIT, UNIT), UNIT)
            values = rows_ref[where, :]
            contract = (((1,), (1,)), ((), ()))
            total = lax.dot_general(
                values, low[node], contract, preferred_element_type=jnp.float32
            ) + lax.dot_general(values, high[node], contract, preferred_element_type=jnp.float32)
            out_ref[level, where, :] = total.astype(jnp.bfloat16)


def make_bases(index, grams, rows, levels):
    nodes, width = grams.shape[0], rows.shape[1]
    return pl.pallas_call(
        basis_kernel,
        out_shape=jax.ShapeDtypeStruct((levels, rows.shape[0], width), jnp.bfloat16),
        in_specs=[
            pl.BlockSpec(memory_space=pltpu.SMEM),
            pl.BlockSpec(memory_space=pltpu.VMEM),
            pl.BlockSpec(memory_space=pltpu.VMEM),
        ],
        out_specs=pl.BlockSpec(memory_space=pltpu.VMEM),
        scratch_shapes=[
            pltpu.VMEM((nodes, width, 2 * width), jnp.float32),
            pltpu.VMEM((nodes, BLOCK, 2 * BLOCK), jnp.float32),
            pltpu.VMEM((nodes, width, width), jnp.bfloat16),
            pltpu.VMEM((nodes, width, width), jnp.bfloat16),
        ],
        compiler_params=pltpu.CompilerParams(vmem_limit_bytes=40 * 2**20),
    )(index, grams, rows)


def running_sum(values):
    length = values.shape[-1]
    step = 1
    while step < length:
        pad = [(0, 0)] * (values.ndim - 1) + [(step, 0)]
        values = values + jnp.pad(values, pad)[..., :length]
        step *= 2
    return values


def to_tree_order(sample, tree_perm):
    rows_dev, width = sample.shape
    devices = tree_perm.shape[0] // rows_dev
    device = lax.axis_index(("row", "col"))
    capacity = (rows_dev + devices - 1) // devices
    grid = tree_perm.reshape(devices, rows_dev)
    mine = grid // rows_dev == device
    rank = running_sum(mine.astype(jnp.int32)) - 1
    slots = jnp.arange(capacity, dtype=jnp.int32)
    chosen = mine[:, None, :] & (rank[:, None, :] == slots[None, :, None])
    send = jnp.sum(jnp.where(chosen, (grid % rows_dev)[:, None, :], 0), axis=2).reshape(-1)
    outgoing = jnp.take(sample, send, axis=0, mode="clip")
    incoming = lax.all_to_all(outgoing, ("row", "col"), split_axis=0, concat_axis=0, tiled=True)
    wanted = lax.dynamic_slice_in_dim(tree_perm, device * rows_dev, rows_dev)
    source = wanted // rows_dev
    order = jnp.arange(rows_dev, dtype=jnp.int32)
    ahead = (source[None, :] == source[:, None]) & (order[None, :] < order[:, None])
    pick = source * capacity + jnp.sum(ahead, axis=1)
    return jnp.take(incoming, pick, axis=0, mode="clip")


def bases_of(sample, tree_perm, leaf_units):
    rows_dev, width = sample.shape
    devices = tree_perm.shape[0] // rows_dev
    device = lax.axis_index(("row", "col"))
    tree_rows = to_tree_order(sample, tree_perm)
    sizes = UNIT * (MINU - 1 + leaf_units)
    leaves = sizes.shape[0]
    ends = running_sum(sizes)
    levels = LEVELS + 1
    units = rows_dev // UNIT
    starts = jnp.arange(devices, dtype=jnp.int32) * rows_dev
    first_leaf = jnp.sum(starts[:, None] >= ends[None, :], axis=1)
    last_leaf = jnp.sum((starts + rows_dev - 1)[:, None] >= ends[None, :], axis=1)
    unit_start = device * rows_dev + jnp.arange(units, dtype=jnp.int32) * UNIT
    unit_leaf = jnp.sum(unit_start[:, None] >= ends[None, :], axis=1)

    reach = [2 + max(rows_dev - 2 * UNIT, 0) // (UNIT * MINU * 2**t) for t in range(levels)]
    half = width // 2
    slots = [(level, which) for level in range(levels) for which in range(reach[level])]
    first = jnp.take(first_leaf, device)
    touched = first + jnp.arange(reach[0], dtype=jnp.int32)
    unit_mask = (unit_leaf[None, :] == touched[:, None]).astype(jnp.bfloat16)
    mask = jnp.repeat(unit_mask, UNIT, axis=1)
    packed = []
    for which in range(reach[0]):
        full = lax.dot_general(
            tree_rows * mask[which][:, None],
            tree_rows,
            (((0,), (0,)), ((), ())),
            preferred_element_type=jnp.float32,
        )
        part = jnp.concatenate([full[:half, :half], full[:half, half:], full[half:, half:]], axis=0)
        packed.append(part.reshape(devices, -1, half))
    outgoing = jnp.concatenate(packed, axis=1)
    incoming = lax.all_to_all(outgoing, ("row", "col"), split_axis=0, concat_axis=0, tiled=True)
    incoming = incoming.reshape(devices * reach[0], -1)
    part_leaf = (first_leaf[:, None] + jnp.arange(reach[0], dtype=jnp.int32)).reshape(-1)
    chosen = jnp.stack(
        [
            part_leaf[None, :] // 2**level == (first_leaf // 2**level + which)[:, None]
            for level, which in slots
        ],
        axis=1,
    )
    sums = jnp.dot(
        chosen.astype(jnp.float32).reshape(devices * len(slots), -1),
        incoming,
        preferred_element_type=jnp.float32,
        precision=HIGHEST,
    )
    sums = sums.reshape(devices, -1, half)
    wanted = lax.all_to_all(sums, ("row", "col"), split_axis=0, concat_axis=0, tiled=True)
    wanted = wanted.reshape(devices, len(slots), -1, half).swapaxes(0, 1)
    wanted = list(wanted.reshape(len(slots), 3 * half, half))

    slot = 0
    last = jnp.take(last_leaf, device)
    unit_half = jnp.eye(half, dtype=jnp.float32)
    eye = jnp.concatenate([unit_half, jnp.zeros_like(unit_half), unit_half], axis=0)
    index = []
    for level in range(levels):
        group = 2**level
        node_sizes = sizes.reshape(leaves // group, group).sum(axis=1)
        low, high = first // group, last // group
        for which in range(reach[level]):
            node = low + which
            rows = jnp.take(node_sizes, jnp.minimum(node, leaves // group - 1))
            mean = wanted[slot + which] / rows.astype(jnp.float32)
            wanted[slot + which] = jnp.where(node <= high, mean, eye)
        index.append(slot + unit_leaf // group - low)
        slot += reach[level]
    return make_bases(jnp.concatenate(index), jnp.stack(wanted), tree_rows, levels)


def shards(kernel, random_cols, tree_perm, leaf_units):
    width = random_cols.shape[1]
    parts = lax.axis_size("row")
    partial_w = lax.dot_general(
        kernel, random_cols, (((0,), (0,)), ((), ())), preferred_element_type=jnp.float32
    ).astype(jnp.bfloat16)
    pieces = lax.all_to_all(partial_w, "row", split_axis=0, concat_axis=0, tiled=True)
    piece = jnp.sum(pieces.reshape(parts, -1, width).astype(jnp.float32), axis=0)
    sample_w = lax.all_gather(piece.astype(jnp.bfloat16), "row", axis=0, tiled=True)
    return bases_of(reduce_panels(kernel, sample_w), tree_perm, leaf_units)


def reduce_panels(kernel, sample_w):
    columns = lax.axis_size("col")
    me = lax.axis_index("col")
    rows_dev = kernel.shape[0] // columns
    ring = columns // 2
    place, side = me // 2, me % 2
    swap = [(i, i ^ 1) for i in range(columns)]
    ahead = [(i, (i + 2) % columns) for i in range(columns)]
    owned = []
    for step in range(ring):
        target = lax.rem(place + ring - 1 - step, ring)
        panel = lax.dynamic_slice_in_dim(kernel, target * 2 * rows_dev, 2 * rows_dev)
        product = jnp.dot(panel, sample_w, preferred_element_type=jnp.float32)
        lower, upper = product[:rows_dev], product[rows_dev:]
        theirs = jnp.where(side == 0, upper, lower).astype(jnp.bfloat16)
        mine = jnp.where(side == 0, lower, upper)
        owned.append((mine, lax.ppermute(theirs, "col", swap)))
    total = None
    for mine, theirs in owned:
        here = mine + theirs.astype(jnp.float32)
        if total is not None:
            here = here + lax.ppermute(total, "col", ahead).astype(jnp.float32)
        total = here.astype(jnp.bfloat16)
    return total


def solution(mesh):
    return jax.shard_map(
        shards,
        mesh=mesh,
        in_specs=(P("row", "col"), P("row", None), P(), P()),
        out_specs=P(None, ("row", "col"), None),
        check_vma=False,
    )
```

```python
import functools

import jax
import jax.numpy as jnp
from jax import lax
from jax.experimental import pallas as pl
from jax.experimental.pallas import tpu as pltpu
from jax.sharding import PartitionSpec as P

UNIT = 128
MINU = 4
MOSTU = 8
LEVELS = 3
BLOCK = 64
HIGHEST = lax.Precision.HIGHEST


def basis_kernel(index_ref, gram_ref, rows_ref, out_ref, work, block, high, low):
    nodes, _, half = gram_ref.shape
    width = 2 * half
    count = width // BLOCK
    eye = (
        lax.broadcasted_iota(jnp.int32, (width, width), 0)
        == lax.broadcasted_iota(jnp.int32, (width, width), 1)
    ).astype(jnp.float32)

    @pl.loop(0, nodes)
    def _(node):
        work[node, :half, :half] = gram_ref[node, :half, :]
        work[node, :half, half:width] = gram_ref[node, half:width, :]
        work[node, half:, :half] = jnp.zeros((half, half), jnp.float32)
        work[node, half:, half:width] = gram_ref[node, width:, :]
        work[node, :, width:] = eye

    small = (
        lax.broadcasted_iota(jnp.int32, (nodes, BLOCK, BLOCK), 1)
        == lax.broadcasted_iota(jnp.int32, (nodes, BLOCK, BLOCK), 2)
    )

    @pl.loop(0, count)
    def _(step):
        for which in range(count):

            @pl.when(step == which)
            def _():
                start = which * BLOCK
                block[:, :, :BLOCK] = work[:, start : start + BLOCK, start : start + BLOCK]
                block[:, :, BLOCK:] = small.astype(jnp.float32)

        for column in range(BLOCK - 1):
            base = column // 8 * 8
            rest = block[:, base:, :]
            pivot_row = rest[:, column - base : column - base + 1, :]
            scale = 1.0 / pivot_row[:, :, column : column + 1]
            below = (
                lax.broadcasted_iota(jnp.int32, (nodes, BLOCK - base, 1), 1) > column - base
            )
            factor = jnp.where(below, rest[:, :, column : column + 1], 0.0)
            block[:, base:, :] = rest - factor * (pivot_row * scale)
        pivots = jnp.sum(jnp.where(small, block[:, :, :BLOCK], 0.0), axis=2, keepdims=True)
        block[:, :, BLOCK:] = block[:, :, BLOCK:] * lax.rsqrt(pivots)

        for which in range(count):

            @pl.when(step == which)
            def _():
                start = which * BLOCK
                after = start + BLOCK
                left = start // 128 * 128
                right = width + (after + 127) // 128 * 128

                @pl.loop(0, nodes)
                def _(node):
                    inverse = block[node][:, BLOCK:]
                    solved = jnp.dot(
                        inverse,
                        work[node, start:after, left:right],
                        preferred_element_type=jnp.float32,
                        precision=HIGHEST,
                    )
                    work[node, start:after, left:right] = solved
                    if after < width:
                        panel = solved[:, : width - left].T
                        change = jnp.dot(
                            panel[after - left :, :],
                            solved,
                            preferred_element_type=jnp.float32,
                            precision=HIGHEST,
                        )
                        work[node, after:, left:right] = work[node, after:, left:right] - change

    @pl.loop(0, nodes)
    def _(node):
        full = work[node, :, width:]
        top = full.astype(jnp.bfloat16)
        high[node] = top
        low[node] = (full - top.astype(jnp.float32)).astype(jnp.bfloat16)

    levels, rows, _ = out_ref.shape
    units = rows // UNIT

    @pl.loop(0, levels)
    def _(level):
        @pl.loop(0, units)
        def _(unit):
            node = index_ref[level * units + unit]
            where = pl.ds(pl.multiple_of(unit * UNIT, UNIT), UNIT)
            values = rows_ref[where, :]
            contract = (((1,), (1,)), ((), ()))
            total = lax.dot_general(
                values, low[node], contract, preferred_element_type=jnp.float32
            ) + lax.dot_general(values, high[node], contract, preferred_element_type=jnp.float32)
            out_ref[level, where, :] = total.astype(jnp.bfloat16)


def make_bases(index, grams, rows, levels):
    nodes, width = grams.shape[0], rows.shape[1]
    return pl.pallas_call(
        basis_kernel,
        out_shape=jax.ShapeDtypeStruct((levels, rows.shape[0], width), jnp.bfloat16),
        in_specs=[
            pl.BlockSpec(memory_space=pltpu.SMEM),
            pl.BlockSpec(memory_space=pltpu.VMEM),
            pl.BlockSpec(memory_space=pltpu.VMEM),
        ],
        out_specs=pl.BlockSpec(memory_space=pltpu.VMEM),
        scratch_shapes=[
            pltpu.VMEM((nodes, width, 2 * width), jnp.float32),
            pltpu.VMEM((nodes, BLOCK, 2 * BLOCK), jnp.float32),
            pltpu.VMEM((nodes, width, width), jnp.bfloat16),
            pltpu.VMEM((nodes, width, width), jnp.bfloat16),
        ],
        compiler_params=pltpu.CompilerParams(vmem_limit_bytes=40 * 2**20),
    )(index, grams, rows)


def running_sum(values):
    length = values.shape[-1]
    step = 1
    while step < length:
        pad = [(0, 0)] * (values.ndim - 1) + [(step, 0)]
        values = values + jnp.pad(values, pad)[..., :length]
        step *= 2
    return values


MESH = pl.DeviceIdType.MESH
SLOTS = 3


def each(count, body):
    def step(index, carry):
        body(index)
        return carry

    lax.fori_loop(0, count, step, 0)


def sketch_kernel(
    sizes,
    k_ref,
    r_ref,
    order_ref,
    out_ref,
    wide,
    tall,
    rt,
    wt,
    w,
    acc,
    own,
    core_out,
    core_in,
    x_out,
    x_in,
    orders,
    product,
    pick,
    y_out,
    y_in,
    z_sum,
    z_out,
    z_own,
    z_in,
    r_out,
    r_in,
    wide_sem,
    tall_sem,
    order_sems,
    core_sems,
    x_sems,
    back_sems,
    y_sems,
    z_sems,
    r_sems,
):
    rows, cols, ys, cap, spread = sizes
    zs = cols // ys
    row, col = lax.axis_index("row"), lax.axis_index("col")
    z, y = lax.div(col, ys), lax.rem(col, ys)
    chunks, width, chunk = wt.shape
    half = width // 2
    blocks, rows_dev, _ = y_out.shape
    part = tall.shape[1]
    subs = rows_dev // part
    core = lax.rem(row, 2)
    pair = row + 1 - 2 * core
    xs = rows // 2
    mine = pl.ds(pl.multiple_of(core * half, half), half)
    other = pl.ds(pl.multiple_of(half - core * half, half), half)

    def wide_copy(step):
        slot = lax.rem(step, SLOTS)
        where = pl.ds(pl.multiple_of(step * chunk, chunk), chunk)
        return pltpu.make_async_copy(k_ref.at[:, where], wide.at[slot], wide_sem.at[slot])

    def tall_copy(step):
        slot = lax.rem(step, SLOTS)
        where = pl.ds(pl.multiple_of(step * part, part), part)
        return pltpu.make_async_copy(k_ref.at[where, :], tall.at[slot], tall_sem.at[slot])

    def send(source, target, sems, index, device):
        return pltpu.make_async_remote_copy(
            src_ref=source,
            dst_ref=target,
            send_sem=sems.at[(0, *index)],
            recv_sem=sems.at[(1, *index)],
            device_id=device,
            device_id_type=MESH,
        )

    def order_copy(away):
        device = (row, lax.rem(col + away, cols))
        return send(order_ref, orders.at[col], order_sems, (away - 1,), device)

    def core_copy(step):
        return send(core_out.at[step], core_in.at[step], core_sems, (step,), (pair, col))

    def x_copy(step, away):
        device = (lax.rem(row + 2 * away, rows), col)
        return send(x_out.at[step], x_in.at[away - 1, step], x_sems, (away - 1, step), device)

    def back_copy(step):
        where = wt.at[step, mine, :]
        return send(where, where, back_sems, (step,), (pair, col))

    y_rows, z_rows = rows_dev // ys, rows_dev // cols

    def y_copy(step, away):
        target = lax.rem(y + away, ys)
        where = pl.ds(pl.multiple_of(target * y_rows, y_rows), y_rows)
        device = (row, z * ys + target)
        return send(
            y_out.at[step, where, :], y_in.at[away - 1, step], y_sems, (away - 1, step), device
        )

    def z_copy(step, away):
        target = lax.rem(z + away, zs)
        where = pl.ds(pl.multiple_of(target * z_rows, z_rows), z_rows)
        device = (row, target * ys + y)
        return send(
            z_out.at[step, where, :], z_in.at[away - 1, step], z_sems, (away - 1, step), device
        )

    def r_copy(step, away):
        target = lax.rem(row + away, rows)
        where = pl.ds(pl.multiple_of(target * cap, cap), cap)
        return send(
            r_out.at[step, where, :],
            r_in.at[row, step],
            r_sems,
            (away - 1, step),
            (target, col),
        )

    for step in range(SLOTS):
        wide_copy(step).start()

    barrier = pltpu.get_barrier_semaphore()
    for away in range(1, rows):
        device = (lax.rem(row + away, rows), col)
        pl.semaphore_signal(barrier, inc=1, device_id=device, device_id_type=MESH)
    for away in range(1, cols):
        device = (row, lax.rem(col + away, cols))
        pl.semaphore_signal(barrier, inc=1, device_id=device, device_id_type=MESH)

    def turn(step):
        where = pl.ds(pl.multiple_of(step * 512, 512), 512)
        rt[:, where] = r_ref[where, :].T

    each(r_ref.shape[0] // 512, turn)
    pl.semaphore_wait(barrier, rows + cols - 2)
    for away in range(1, cols):
        order_copy(away).start()
    orders[col] = order_ref[...]

    def first(step):
        @pl.when(step < chunks)
        def _():
            wide_copy(step).wait()
            acc[...] = jnp.dot(
                rt[...], wide[lax.rem(step, SLOTS)], preferred_element_type=jnp.float32
            )

            @pl.when(step + SLOTS < chunks)
            def _():
                wide_copy(step + SLOTS).start()

            core_out[step] = acc[other, :].astype(jnp.bfloat16)
            own[step] = acc[mine, :]
            core_copy(step).start()

        @pl.when(step == chunks - 1)
        def _():
            for ahead in range(SLOTS):
                tall_copy(ahead).start()

        @pl.when((step >= 1) & (step <= chunks))
        def _():
            here = step - 1
            core_copy(here).wait()
            total = own[here] + core_in[here].astype(jnp.float32)
            own[here] = total
            x_out[here] = total.astype(jnp.bfloat16)
            for away in range(1, xs):
                x_copy(here, away).start()

        @pl.when((step >= 3) & (step <= chunks + 2))
        def _():
            here = step - 3
            total = own[here]
            for away in range(1, xs):
                x_copy(here, away).wait()
                total = total + x_in[away - 1, here].astype(jnp.float32)
            wt[here, mine, :] = total.astype(jnp.bfloat16)
            back_copy(here).start()

        @pl.when(step >= 4)
        def _():
            here = step - 4
            back_copy(here).wait()
            w[pl.ds(pl.multiple_of(here * chunk, chunk), chunk), :] = wt[here].T

    each(chunks + 4, first)
    for away in range(1, cols):
        order_copy(away).wait()

    lane = lax.broadcasted_iota(jnp.int32, (128, 128), 1).astype(jnp.float32)

    def second(step):
        @pl.when(step < blocks)
        def _():
            for sub in range(subs):
                index = step * subs + sub
                tall_copy(index).wait()
                product[sub * part : (sub + 1) * part, :] = jnp.dot(
                    tall[lax.rem(index, SLOTS)], w[...], preferred_element_type=jnp.float32
                ).astype(jnp.bfloat16)

                @pl.when(index + SLOTS < blocks * subs)
                def _():
                    tall_copy(index + SLOTS).start()

            for piece in range(rows_dev // 128):
                wanted = jnp.broadcast_to(orders[step, piece : piece + 1, :], (128, 128)).T
                for tile in range(rows_dev // 128):
                    hit = jnp.where(wanted == lane + 128.0 * tile, 1.0, 0.0)
                    pick[piece * 128 : (piece + 1) * 128, tile * 128 : (tile + 1) * 128] = (
                        hit.astype(jnp.bfloat16)
                    )
            y_out[step] = jnp.dot(
                pick[...], product[...], preferred_element_type=jnp.float32
            ).astype(jnp.bfloat16)
            for away in range(1, ys):
                y_copy(step, away).start()

        @pl.when((step >= 1) & (step <= blocks))
        def _():
            here = step - 1
            kept = pl.ds(pl.multiple_of(y * y_rows, y_rows), y_rows)
            total = y_out[here, kept, :].astype(jnp.float32)
            for away in range(1, ys):
                y_copy(here, away).wait()
                total = total + y_in[away - 1, here].astype(jnp.float32)
            z_sum[...] = total
            z_out[here] = total.astype(jnp.bfloat16)
            z_own[here] = z_sum[pl.ds(pl.multiple_of(z * z_rows, z_rows), z_rows), :]
            for away in range(1, zs):
                z_copy(here, away).start()

        @pl.when(step >= 3)
        def _():
            here = step - 3
            total = z_own[here]
            for away in range(1, zs):
                z_copy(here, away).wait()
                total = total + z_in[away - 1, here].astype(jnp.float32)
            if not spread:
                out_ref[here] = total.astype(jnp.bfloat16)
            else:
                r_out[here] = total.astype(jnp.bfloat16)
                for away in range(1, rows):
                    r_copy(here, away).start()

    each(blocks + 3, second)
    if spread:
        kept = pl.ds(pl.multiple_of(row * cap, cap), cap)
        r_in[row] = r_out[:, kept, :]

        def last(step):
            for away in range(1, rows):
                r_copy(step, away).wait()

        each(blocks, last)
        out_ref[...] = r_in[...]


def sketch(kernel, random_cols, order):
    height, length = kernel.shape
    width = random_cols.shape[1]
    rows, cols = lax.axis_size("row"), lax.axis_size("col")
    rows_dev = height // cols
    ys = max(cols // 4, 1)
    zs = cols // ys
    cap = rows_dev // (rows * cols)
    spread = cap % 16 == 0
    chunk = min(256, length)
    chunks = length // chunk
    part = min(512, rows_dev)
    half = width // 2
    y_rows, z_rows = rows_dev // ys, rows_dev // cols
    bf, f32 = jnp.bfloat16, jnp.float32
    shape = (rows, cols, cap, width) if spread else (cols, z_rows, width)
    peers = max(rows // 2 - 1, 1)
    dma = pltpu.SemaphoreType.DMA
    got = pl.pallas_call(
        functools.partial(sketch_kernel, (rows, cols, ys, cap, spread)),
        out_shape=jax.ShapeDtypeStruct(shape, bf),
        in_specs=[
            pl.BlockSpec(memory_space=pl.ANY),
            pl.BlockSpec(memory_space=pltpu.VMEM),
            pl.BlockSpec(memory_space=pltpu.VMEM),
        ],
        out_specs=pl.BlockSpec(memory_space=pltpu.VMEM),
        scratch_shapes=[
            pltpu.VMEM((SLOTS, height, chunk), bf),
            pltpu.VMEM((SLOTS, part, length), bf),
            pltpu.VMEM((width, height), bf),
            pltpu.VMEM((chunks, width, chunk), bf),
            pltpu.VMEM((length, width), bf),
            pltpu.VMEM((width, chunk), f32),
            pltpu.VMEM((chunks, half, chunk), f32),
            pltpu.VMEM((chunks, half, chunk), bf),
            pltpu.VMEM((chunks, half, chunk), bf),
            pltpu.VMEM((chunks, half, chunk), bf),
            pltpu.VMEM((peers, chunks, half, chunk), bf),
            pltpu.VMEM((cols, *order.shape), f32),
            pltpu.VMEM((rows_dev, width), bf),
            pltpu.VMEM((rows_dev, rows_dev), bf),
            pltpu.VMEM((cols, rows_dev, width), bf),
            pltpu.VMEM((max(ys - 1, 1), cols, y_rows, width), bf),
            pltpu.VMEM((y_rows, width), f32),
            pltpu.VMEM((cols, y_rows, width), bf),
            pltpu.VMEM((cols, z_rows, width), f32),
            pltpu.VMEM((zs - 1, cols, z_rows, width), bf),
            pltpu.VMEM((cols, z_rows, width), bf),
            pltpu.VMEM((rows, cols, cap if spread else 16, width), bf),
            dma((SLOTS,)),
            dma((SLOTS,)),
            dma((2, cols - 1)),
            dma((2, chunks)),
            dma((2, peers, chunks)),
            dma((2, chunks)),
            dma((2, max(ys - 1, 1), cols)),
            dma((2, zs - 1, cols)),
            dma((2, rows - 1, cols)),
        ],
        compiler_params=pltpu.CompilerParams(
            collective_id=0, has_side_effects=True, vmem_limit_bytes=60 * 2**20
        ),
        cost_estimate=pl.CostEstimate(
            flops=4 * height * length * width,
            bytes_accessed=4 * height * length,
            transcendentals=0,
        ),
    )(kernel, random_cols, order)
    if spread:
        return got.reshape(rows_dev, width)
    got = got.reshape(cols, rows, cap, width).swapaxes(0, 1).reshape(rows_dev, width)
    return lax.all_to_all(got, "row", split_axis=0, concat_axis=0, tiled=True)


def send_order(tree_perm, rows_dev):
    rows, cols = lax.axis_size("row"), lax.axis_size("col")
    ys = max(cols // 4, 1)
    devices = rows * cols
    device = lax.axis_index(("row", "col"))
    capacity = rows_dev // devices
    grid = tree_perm.reshape(devices, rows_dev)
    mine = grid // rows_dev == device
    rank = running_sum(mine.astype(jnp.int32)) - 1
    slots = jnp.arange(capacity, dtype=jnp.int32)
    chosen = mine[:, None, :] & (rank[:, None, :] == slots[None, :, None])
    order = jnp.sum(jnp.where(chosen, (grid % rows_dev)[:, None, :], 0), axis=2)
    order = order.reshape(rows, cols // ys, ys, capacity).transpose(2, 1, 0, 3)
    order = order.reshape(rows_dev // 128, 128).astype(jnp.float32)
    return jnp.pad(order, ((0, -order.shape[0] % 8), (0, 0)))


def in_tree_order(incoming, tree_perm):
    rows_dev = incoming.shape[0]
    devices = tree_perm.shape[0] // rows_dev
    device = lax.axis_index(("row", "col"))
    capacity = rows_dev // devices
    wanted = lax.dynamic_slice_in_dim(tree_perm, device * rows_dev, rows_dev)
    source = wanted // rows_dev
    order = jnp.arange(rows_dev, dtype=jnp.int32)
    ahead = (source[None, :] == source[:, None]) & (order[None, :] < order[:, None])
    pick = source * capacity + jnp.sum(ahead, axis=1)
    return jnp.take(incoming, pick, axis=0, mode="clip")


def bases_of(tree_rows, tree_perm, leaf_units):
    rows_dev, width = tree_rows.shape
    devices = tree_perm.shape[0] // rows_dev
    device = lax.axis_index(("row", "col"))
    sizes = UNIT * (MINU - 1 + leaf_units)
    leaves = sizes.shape[0]
    ends = running_sum(sizes)
    levels = LEVELS + 1
    units = rows_dev // UNIT
    starts = jnp.arange(devices, dtype=jnp.int32) * rows_dev
    first_leaf = jnp.sum(starts[:, None] >= ends[None, :], axis=1)
    last_leaf = jnp.sum((starts + rows_dev - 1)[:, None] >= ends[None, :], axis=1)
    unit_start = device * rows_dev + jnp.arange(units, dtype=jnp.int32) * UNIT
    unit_leaf = jnp.sum(unit_start[:, None] >= ends[None, :], axis=1)

    reach = [2 + max(rows_dev - 2 * UNIT, 0) // (UNIT * MINU * 2**t) for t in range(levels)]
    half = width // 2
    slots = [(level, which) for level in range(levels) for which in range(reach[level])]
    first = jnp.take(first_leaf, device)
    touched = first + jnp.arange(reach[0], dtype=jnp.int32)
    unit_mask = (unit_leaf[None, :] == touched[:, None]).astype(jnp.bfloat16)
    mask = jnp.repeat(unit_mask, UNIT, axis=1)
    packed = []
    for which in range(reach[0]):
        full = lax.dot_general(
            tree_rows * mask[which][:, None],
            tree_rows,
            (((0,), (0,)), ((), ())),
            preferred_element_type=jnp.float32,
        )
        part = jnp.concatenate([full[:half, :half], full[:half, half:], full[half:, half:]], axis=0)
        packed.append(part.reshape(devices, -1, half))
    outgoing = jnp.concatenate(packed, axis=1)
    incoming = lax.all_to_all(outgoing, ("row", "col"), split_axis=0, concat_axis=0, tiled=True)
    incoming = incoming.reshape(devices * reach[0], -1)
    part_leaf = (first_leaf[:, None] + jnp.arange(reach[0], dtype=jnp.int32)).reshape(-1)
    chosen = jnp.stack(
        [
            part_leaf[None, :] // 2**level == (first_leaf // 2**level + which)[:, None]
            for level, which in slots
        ],
        axis=1,
    )
    sums = jnp.dot(
        chosen.astype(jnp.float32).reshape(devices * len(slots), -1),
        incoming,
        preferred_element_type=jnp.float32,
        precision=HIGHEST,
    )
    sums = sums.reshape(devices, -1, half)
    wanted = lax.all_to_all(sums, ("row", "col"), split_axis=0, concat_axis=0, tiled=True)
    wanted = wanted.reshape(devices, len(slots), -1, half).swapaxes(0, 1)
    wanted = list(wanted.reshape(len(slots), 3 * half, half))

    slot = 0
    last = jnp.take(last_leaf, device)
    unit_half = jnp.eye(half, dtype=jnp.float32)
    eye = jnp.concatenate([unit_half, jnp.zeros_like(unit_half), unit_half], axis=0)
    index = []
    for level in range(levels):
        group = 2**level
        node_sizes = sizes.reshape(leaves // group, group).sum(axis=1)
        low, high = first // group, last // group
        for which in range(reach[level]):
            node = low + which
            rows = jnp.take(node_sizes, jnp.minimum(node, leaves // group - 1))
            mean = wanted[slot + which] / rows.astype(jnp.float32)
            wanted[slot + which] = jnp.where(node <= high, mean, eye)
        index.append(slot + unit_leaf // group - low)
        slot += reach[level]
    return make_bases(jnp.concatenate(index), jnp.stack(wanted), tree_rows, levels)


def shards(kernel, random_cols, tree_perm, leaf_units):
    rows_dev = kernel.shape[0] // lax.axis_size("col")
    incoming = sketch(kernel, random_cols, send_order(tree_perm, rows_dev))
    return bases_of(in_tree_order(incoming, tree_perm), tree_perm, leaf_units)


def solution(mesh):
    return jax.shard_map(
        shards,
        mesh=mesh,
        in_specs=(P("row", "col"), P("row", None), P(), P()),
        out_specs=P(None, ("row", "col"), None),
        check_vma=False,
    )
```

```python
import functools

import jax
import jax.numpy as jnp
from jax import lax
from jax.experimental import pallas as pl
from jax.experimental.pallas import tpu as pltpu
from jax.sharding import PartitionSpec as P

UNIT = 128
MINU = 4
MOSTU = 8
LEVELS = 3
BLOCK = 64
HIGHEST = lax.Precision.HIGHEST


def basis_kernel(index_ref, gram_ref, rows_ref, out_ref, work, block, high, low):
    nodes, _, half = gram_ref.shape
    width, fourth = 2 * half, half // 2
    count = width // BLOCK
    eye = (
        lax.broadcasted_iota(jnp.int32, (width, width), 0)
        == lax.broadcasted_iota(jnp.int32, (width, width), 1)
    ).astype(jnp.float32)

    @pl.loop(0, nodes)
    def _(node):
        corners = gram_ref[node, fourth:half, :]
        work[node, :half, :half] = gram_ref[node, :half, :]
        work[node, :half, half:width] = gram_ref[node, width - fourth :, :]
        work[node, half:, :half] = jnp.zeros((half, half), jnp.float32)
        work[node, half : width - fourth, half:width] = gram_ref[node, half : width - fourth, :]
        swapped = [corners[:, fourth:], corners[:, :fourth]]
        work[node, width - fourth :, half:width] = jnp.concatenate(swapped, axis=1)
        work[node, :, width:] = eye

    small = (
        lax.broadcasted_iota(jnp.int32, (nodes, BLOCK, BLOCK), 1)
        == lax.broadcasted_iota(jnp.int32, (nodes, BLOCK, BLOCK), 2)
    )

    @pl.loop(0, count)
    def _(step):
        for which in range(count):

            @pl.when(step == which)
            def _():
                start = which * BLOCK
                block[:, :, :BLOCK] = work[:, start : start + BLOCK, start : start + BLOCK]
                block[:, :, BLOCK:] = small.astype(jnp.float32)

        for column in range(BLOCK - 1):
            base = column // 8 * 8
            rest = block[:, base:, :]
            pivot_row = rest[:, column - base : column - base + 1, :]
            scale = 1.0 / pivot_row[:, :, column : column + 1]
            below = (
                lax.broadcasted_iota(jnp.int32, (nodes, BLOCK - base, 1), 1) > column - base
            )
            factor = jnp.where(below, rest[:, :, column : column + 1], 0.0)
            block[:, base:, :] = rest - factor * (pivot_row * scale)
        pivots = jnp.sum(jnp.where(small, block[:, :, :BLOCK], 0.0), axis=2, keepdims=True)
        block[:, :, BLOCK:] = block[:, :, BLOCK:] * lax.rsqrt(pivots)

        for which in range(count):

            @pl.when(step == which)
            def _():
                start = which * BLOCK
                after = start + BLOCK
                left = start // 128 * 128
                right = width + (after + 127) // 128 * 128

                @pl.loop(0, nodes, unroll=True)
                def _(node):
                    inverse = block[node][:, BLOCK:]
                    solved = jnp.dot(
                        inverse,
                        work[node, start:after, left:right],
                        preferred_element_type=jnp.float32,
                        precision=HIGHEST,
                    )
                    work[node, start:after, left:right] = solved
                    if after < width:
                        panel = solved[:, : width - left].T
                        change = jnp.dot(
                            panel[after - left :, :],
                            solved,
                            preferred_element_type=jnp.float32,
                            precision=HIGHEST,
                        )
                        work[node, after:, left:right] = work[node, after:, left:right] - change

    @pl.loop(0, nodes, unroll=True)
    def _(node):
        full = work[node, :, width:]
        top = full.astype(jnp.bfloat16)
        high[node] = top
        low[node] = (full - top.astype(jnp.float32)).astype(jnp.bfloat16)

    levels, rows, _ = out_ref.shape
    units = rows // UNIT

    @pl.loop(0, levels)
    def _(level):
        @pl.loop(0, units, unroll=True)
        def _(unit):
            node = index_ref[level * units + unit]
            where = pl.ds(pl.multiple_of(unit * UNIT, UNIT), UNIT)
            values = rows_ref[where, :]
            contract = (((1,), (1,)), ((), ()))
            total = lax.dot_general(
                values, low[node], contract, preferred_element_type=jnp.float32
            ) + lax.dot_general(values, high[node], contract, preferred_element_type=jnp.float32)
            out_ref[level, where, :] = total.astype(jnp.bfloat16)


def make_bases(index, grams, rows, levels):
    nodes, width = grams.shape[0], rows.shape[1]
    return pl.pallas_call(
        basis_kernel,
        out_shape=jax.ShapeDtypeStruct((levels, rows.shape[0], width), jnp.bfloat16),
        in_specs=[
            pl.BlockSpec(memory_space=pltpu.SMEM),
            pl.BlockSpec(memory_space=pltpu.VMEM),
            pl.BlockSpec(memory_space=pltpu.VMEM),
        ],
        out_specs=pl.BlockSpec(memory_space=pltpu.VMEM),
        scratch_shapes=[
            pltpu.VMEM((nodes, width, 2 * width), jnp.float32),
            pltpu.VMEM((nodes, BLOCK, 2 * BLOCK), jnp.float32),
            pltpu.VMEM((nodes, width, width), jnp.bfloat16),
            pltpu.VMEM((nodes, width, width), jnp.bfloat16),
        ],
        compiler_params=pltpu.CompilerParams(vmem_limit_bytes=40 * 2**20),
    )(index, grams, rows)


def running_sum(values):
    length = values.shape[-1]
    before = jnp.arange(length)[:, None] <= jnp.arange(length)[None, :]
    return jnp.sum(jnp.where(before, values[..., :, None], 0), axis=-2)


def running_count(flags):
    count, length = flags.shape
    pieces = length // 128
    before = jnp.arange(128)[:, None] <= jnp.arange(128)[None, :]
    within = jnp.dot(
        flags.reshape(-1, 128).astype(jnp.bfloat16),
        before.astype(jnp.bfloat16),
        preferred_element_type=jnp.float32,
    ).reshape(count, pieces, 128)
    total = within[:, :, 127]
    earlier = running_sum(total) - total
    return (within + earlier[:, :, None]).reshape(count, length).astype(jnp.int32)


MESH = pl.DeviceIdType.MESH
SLOTS = 3


def each(count, body):
    def step(index, carry):
        body(index)
        return carry

    lax.fori_loop(0, count, step, 0)


def sketch_kernel(
    sizes,
    k_ref,
    r_ref,
    order_ref,
    out_ref,
    wide,
    tall,
    rt,
    wt,
    w,
    acc,
    own,
    core_out,
    core_in,
    x_out,
    x_in,
    orders,
    product,
    pick,
    y_out,
    y_in,
    z_sum,
    z_out,
    z_own,
    z_in,
    r_out,
    r_in,
    wide_sem,
    tall_sem,
    order_sems,
    core_sems,
    x_sems,
    back_sems,
    y_sems,
    z_sems,
    r_sems,
):
    rows, cols, ys, cap, spread = sizes
    zs = cols // ys
    row, col = lax.axis_index("row"), lax.axis_index("col")
    z, y = lax.div(col, ys), lax.rem(col, ys)
    chunks, width, chunk = wt.shape
    half = width // 2
    blocks, rows_dev, _ = y_out.shape
    part = tall.shape[1]
    subs = rows_dev // part
    core = lax.rem(row, 2)
    pair = row + 1 - 2 * core
    xs = rows // 2
    mine = pl.ds(pl.multiple_of(core * half, half), half)
    other = pl.ds(pl.multiple_of(half - core * half, half), half)

    def wide_copy(step):
        slot = lax.rem(step, SLOTS)
        where = pl.ds(pl.multiple_of(step * chunk, chunk), chunk)
        return pltpu.make_async_copy(k_ref.at[:, where], wide.at[slot], wide_sem.at[slot])

    def tall_copy(step):
        slot = lax.rem(step, SLOTS)
        where = pl.ds(pl.multiple_of(step * part, part), part)
        return pltpu.make_async_copy(k_ref.at[where, :], tall.at[slot], tall_sem.at[slot])

    def send(source, target, sems, index, device):
        return pltpu.make_async_remote_copy(
            src_ref=source,
            dst_ref=target,
            send_sem=sems.at[(0, *index)],
            recv_sem=sems.at[(1, *index)],
            device_id=device,
            device_id_type=MESH,
        )

    def order_copy(away):
        device = (row, lax.rem(col + away, cols))
        return send(order_ref, orders.at[col], order_sems, (away - 1,), device)

    def core_copy(step):
        return send(core_out.at[step], core_in.at[step], core_sems, (step,), (pair, col))

    def x_copy(step, away):
        device = (lax.rem(row + 2 * away, rows), col)
        return send(x_out.at[step], x_in.at[away - 1, step], x_sems, (away - 1, step), device)

    def back_copy(step):
        where = wt.at[step, mine, :]
        return send(where, where, back_sems, (step,), (pair, col))

    y_rows, z_rows = rows_dev // ys, rows_dev // cols

    def y_copy(step, away):
        target = lax.rem(y + away, ys)
        where = pl.ds(pl.multiple_of(target * y_rows, y_rows), y_rows)
        device = (row, z * ys + target)
        return send(
            y_out.at[step, where, :], y_in.at[away - 1, step], y_sems, (away - 1, step), device
        )

    def z_copy(step, away):
        target = lax.rem(z + away, zs)
        where = pl.ds(pl.multiple_of(target * z_rows, z_rows), z_rows)
        device = (row, target * ys + y)
        return send(
            z_out.at[step, where, :], z_in.at[away - 1, step], z_sems, (away - 1, step), device
        )

    def r_copy(step, away):
        target = lax.rem(row + away, rows)
        where = pl.ds(pl.multiple_of(target * cap, cap), cap)
        return send(
            r_out.at[step, where, :],
            r_in.at[row, step],
            r_sems,
            (away - 1, step),
            (target, col),
        )

    for step in range(SLOTS):
        wide_copy(step).start()

    barrier = pltpu.get_barrier_semaphore()
    for away in range(1, rows):
        device = (lax.rem(row + away, rows), col)
        pl.semaphore_signal(barrier, inc=1, device_id=device, device_id_type=MESH)
    for away in range(1, cols):
        device = (row, lax.rem(col + away, cols))
        pl.semaphore_signal(barrier, inc=1, device_id=device, device_id_type=MESH)

    def turn(step):
        where = pl.ds(pl.multiple_of(step * 512, 512), 512)
        rt[:, where] = r_ref[where, :].T

    each(r_ref.shape[0] // 512, turn)
    pl.semaphore_wait(barrier, rows + cols - 2)
    for away in range(1, cols):
        order_copy(away).start()
    orders[col] = order_ref[...]

    def first(step):
        @pl.when(step < chunks)
        def _():
            wide_copy(step).wait()
            acc[...] = jnp.dot(
                rt[...], wide[lax.rem(step, SLOTS)], preferred_element_type=jnp.float32
            )

            @pl.when(step + SLOTS < chunks)
            def _():
                wide_copy(step + SLOTS).start()

            core_out[step] = acc[other, :].astype(jnp.bfloat16)
            own[step] = acc[mine, :]
            core_copy(step).start()

        @pl.when(step == chunks - 1)
        def _():
            for ahead in range(SLOTS):
                tall_copy(ahead).start()

        @pl.when((step >= 1) & (step <= chunks))
        def _():
            here = step - 1
            core_copy(here).wait()
            total = own[here] + core_in[here].astype(jnp.float32)
            own[here] = total
            x_out[here] = total.astype(jnp.bfloat16)
            for away in range(1, xs):
                x_copy(here, away).start()

        @pl.when((step >= 3) & (step <= chunks + 2))
        def _():
            here = step - 3
            total = own[here]
            for away in range(1, xs):
                x_copy(here, away).wait()
                total = total + x_in[away - 1, here].astype(jnp.float32)
            wt[here, mine, :] = total.astype(jnp.bfloat16)
            back_copy(here).start()

        @pl.when(step >= 4)
        def _():
            here = step - 4
            back_copy(here).wait()
            w[pl.ds(pl.multiple_of(here * chunk, chunk), chunk), :] = wt[here].T

    each(chunks + 4, first)
    for away in range(1, cols):
        order_copy(away).wait()

    lane = lax.broadcasted_iota(jnp.int32, (128, 128), 1).astype(jnp.float32)

    def second(step):
        @pl.when(step < blocks)
        def _():
            for sub in range(subs):
                index = step * subs + sub
                tall_copy(index).wait()
                product[sub * part : (sub + 1) * part, :] = jnp.dot(
                    tall[lax.rem(index, SLOTS)], w[...], preferred_element_type=jnp.float32
                ).astype(jnp.bfloat16)

                @pl.when(index + SLOTS < blocks * subs)
                def _():
                    tall_copy(index + SLOTS).start()

            for piece in range(rows_dev // 128):
                wanted = jnp.broadcast_to(orders[step, piece : piece + 1, :], (128, 128)).T
                for tile in range(rows_dev // 128):
                    hit = jnp.where(wanted == lane + 128.0 * tile, 1.0, 0.0)
                    pick[piece * 128 : (piece + 1) * 128, tile * 128 : (tile + 1) * 128] = (
                        hit.astype(jnp.bfloat16)
                    )
            y_out[step] = jnp.dot(
                pick[...], product[...], preferred_element_type=jnp.float32
            ).astype(jnp.bfloat16)
            for away in range(1, ys):
                y_copy(step, away).start()

        @pl.when((step >= 1) & (step <= blocks))
        def _():
            here = step - 1
            kept = pl.ds(pl.multiple_of(y * y_rows, y_rows), y_rows)
            total = y_out[here, kept, :].astype(jnp.float32)
            for away in range(1, ys):
                y_copy(here, away).wait()
                total = total + y_in[away - 1, here].astype(jnp.float32)
            z_sum[...] = total
            z_out[here] = total.astype(jnp.bfloat16)
            z_own[here] = z_sum[pl.ds(pl.multiple_of(z * z_rows, z_rows), z_rows), :]
            for away in range(1, zs):
                z_copy(here, away).start()

        @pl.when(step >= 3)
        def _():
            here = step - 3
            total = z_own[here]
            for away in range(1, zs):
                z_copy(here, away).wait()
                total = total + z_in[away - 1, here].astype(jnp.float32)
            if not spread:
                out_ref[here] = total.astype(jnp.bfloat16)
            else:
                r_out[here] = total.astype(jnp.bfloat16)
                for away in range(1, rows):
                    r_copy(here, away).start()

    each(blocks + 3, second)
    if spread:
        kept = pl.ds(pl.multiple_of(row * cap, cap), cap)
        r_in[row] = r_out[:, kept, :]

        def last(step):
            for away in range(1, rows):
                r_copy(step, away).wait()

        each(blocks, last)
        out_ref[...] = r_in[...]


def sketch(kernel, random_cols, order):
    height, length = kernel.shape
    width = random_cols.shape[1]
    rows, cols = lax.axis_size("row"), lax.axis_size("col")
    rows_dev = height // cols
    ys = max(cols // 4, 1)
    zs = cols // ys
    cap = rows_dev // (rows * cols)
    spread = cap % 16 == 0
    chunk = min(256, length)
    chunks = length // chunk
    part = min(512, rows_dev)
    half = width // 2
    y_rows, z_rows = rows_dev // ys, rows_dev // cols
    bf, f32 = jnp.bfloat16, jnp.float32
    shape = (rows, cols, cap, width) if spread else (cols, z_rows, width)
    peers = max(rows // 2 - 1, 1)
    dma = pltpu.SemaphoreType.DMA
    got = pl.pallas_call(
        functools.partial(sketch_kernel, (rows, cols, ys, cap, spread)),
        out_shape=jax.ShapeDtypeStruct(shape, bf),
        in_specs=[
            pl.BlockSpec(memory_space=pl.ANY),
            pl.BlockSpec(memory_space=pltpu.VMEM),
            pl.BlockSpec(memory_space=pltpu.VMEM),
        ],
        out_specs=pl.BlockSpec(memory_space=pltpu.VMEM),
        scratch_shapes=[
            pltpu.VMEM((SLOTS, height, chunk), bf),
            pltpu.VMEM((SLOTS, part, length), bf),
            pltpu.VMEM((width, height), bf),
            pltpu.VMEM((chunks, width, chunk), bf),
            pltpu.VMEM((length, width), bf),
            pltpu.VMEM((width, chunk), f32),
            pltpu.VMEM((chunks, half, chunk), f32),
            pltpu.VMEM((chunks, half, chunk), bf),
            pltpu.VMEM((chunks, half, chunk), bf),
            pltpu.VMEM((chunks, half, chunk), bf),
            pltpu.VMEM((peers, chunks, half, chunk), bf),
            pltpu.VMEM((cols, *order.shape), f32),
            pltpu.VMEM((rows_dev, width), bf),
            pltpu.VMEM((rows_dev, rows_dev), bf),
            pltpu.VMEM((cols, rows_dev, width), bf),
            pltpu.VMEM((max(ys - 1, 1), cols, y_rows, width), bf),
            pltpu.VMEM((y_rows, width), f32),
            pltpu.VMEM((cols, y_rows, width), bf),
            pltpu.VMEM((cols, z_rows, width), f32),
            pltpu.VMEM((zs - 1, cols, z_rows, width), bf),
            pltpu.VMEM((cols, z_rows, width), bf),
            pltpu.VMEM((rows, cols, cap if spread else 16, width), bf),
            dma((SLOTS,)),
            dma((SLOTS,)),
            dma((2, cols - 1)),
            dma((2, chunks)),
            dma((2, peers, chunks)),
            dma((2, chunks)),
            dma((2, max(ys - 1, 1), cols)),
            dma((2, zs - 1, cols)),
            dma((2, rows - 1, cols)),
        ],
        compiler_params=pltpu.CompilerParams(
            collective_id=0, has_side_effects=True, vmem_limit_bytes=60 * 2**20
        ),
        cost_estimate=pl.CostEstimate(
            flops=4 * height * length * width,
            bytes_accessed=4 * height * length,
            transcendentals=0,
        ),
    )(kernel, random_cols, order)
    if spread:
        return got.reshape(rows_dev, width)
    got = got.reshape(cols, rows, cap, width).swapaxes(0, 1).reshape(rows_dev, width)
    return lax.all_to_all(got, "row", split_axis=0, concat_axis=0, tiled=True)


def send_order(tree_perm, rows_dev):
    rows, cols = lax.axis_size("row"), lax.axis_size("col")
    ys = max(cols // 4, 1)
    devices = rows * cols
    device = lax.axis_index(("row", "col"))
    capacity = rows_dev // devices
    grid = tree_perm.reshape(devices, rows_dev)
    mine = grid // rows_dev == device
    rank = running_count(mine) - 1
    slots = jnp.arange(capacity, dtype=jnp.int32)
    chosen = mine[:, None, :] & (rank[:, None, :] == slots[None, :, None])
    order = jnp.sum(jnp.where(chosen, (grid % rows_dev)[:, None, :], 0), axis=2)
    order = order.reshape(rows, cols // ys, ys, capacity).transpose(2, 1, 0, 3)
    order = order.reshape(rows_dev // 128, 128).astype(jnp.float32)
    return jnp.pad(order, ((0, -order.shape[0] % 8), (0, 0)))


def in_tree_order(incoming, tree_perm):
    rows_dev = incoming.shape[0]
    devices = tree_perm.shape[0] // rows_dev
    device = lax.axis_index(("row", "col"))
    capacity = rows_dev // devices
    wanted = lax.dynamic_slice_in_dim(tree_perm, device * rows_dev, rows_dev)
    source = wanted // rows_dev
    order = jnp.arange(rows_dev, dtype=jnp.int32)
    ahead = (source[None, :] == source[:, None]) & (order[None, :] < order[:, None])
    pick = source * capacity + jnp.sum(ahead, axis=1)
    return jnp.take(incoming, pick, axis=0, mode="clip")


def bases_of(tree_rows, tree_perm, leaf_units):
    rows_dev, width = tree_rows.shape
    devices = tree_perm.shape[0] // rows_dev
    device = lax.axis_index(("row", "col"))
    sizes = UNIT * (MINU - 1 + leaf_units)
    leaves = sizes.shape[0]
    ends = running_sum(sizes)
    levels = LEVELS + 1
    units = rows_dev // UNIT
    starts = jnp.arange(devices, dtype=jnp.int32) * rows_dev
    first_leaf = jnp.sum(starts[:, None] >= ends[None, :], axis=1)
    last_leaf = jnp.sum((starts + rows_dev - 1)[:, None] >= ends[None, :], axis=1)
    unit_start = device * rows_dev + jnp.arange(units, dtype=jnp.int32) * UNIT
    unit_leaf = jnp.sum(unit_start[:, None] >= ends[None, :], axis=1)

    reach = [2 + max(rows_dev - 2 * UNIT, 0) // (UNIT * MINU * 2**t) for t in range(levels)]
    half, fourth = width // 2, width // 4
    lanes = half if (width + fourth) % devices == 0 else fourth
    slots = [(level, which) for level in range(levels) for which in range(2)]
    first = jnp.take(first_leaf, device)
    touched = first + jnp.arange(reach[0], dtype=jnp.int32)
    unit_mask = (unit_leaf[None, :] == touched[:, None]).astype(jnp.bfloat16)
    mask = jnp.repeat(unit_mask, UNIT, axis=1)
    packed = []
    for which in range(reach[0]):
        full = lax.dot_general(
            tree_rows * mask[which][:, None],
            tree_rows,
            (((0,), (0,)), ((), ())),
            preferred_element_type=jnp.float32,
        )
        corners = [full[-fourth:, -fourth:], full[fourth:half, fourth:half]]
        part = jnp.concatenate(
            [
                full[:fourth, :half],
                jnp.concatenate(corners, axis=1),
                full[half:-fourth, half:],
                full[:half, half:],
            ],
            axis=0,
        )
        packed.append(part)
    outgoing = jnp.concatenate([part.reshape(devices, -1, lanes) for part in packed], axis=1)
    incoming = lax.all_to_all(outgoing, ("row", "col"), split_axis=0, concat_axis=0, tiled=True)
    incoming = incoming.reshape(devices * reach[0], -1)
    part_leaf = (first_leaf[:, None] + jnp.arange(reach[0], dtype=jnp.int32)).reshape(-1)
    chosen = jnp.stack(
        [
            part_leaf[None, :] // 2**level == ((first_leaf, last_leaf)[which] // 2**level)[:, None]
            for level, which in slots
        ],
        axis=1,
    )
    sums = jnp.dot(
        chosen.astype(jnp.float32).reshape(devices * len(slots), -1),
        incoming,
        preferred_element_type=jnp.float32,
        precision=HIGHEST,
    )
    sums = sums.reshape(devices, -1, lanes)
    wanted = lax.all_to_all(sums, ("row", "col"), split_axis=0, concat_axis=0, tiled=True)
    wanted = wanted.reshape(devices, len(slots), -1, lanes).swapaxes(0, 1)
    wanted = wanted.reshape(len(slots), width + fourth, half)

    last = jnp.take(last_leaf, device)
    counts, index = [], []
    for level in range(levels):
        group = 2**level
        node_sizes = sizes.reshape(leaves // group, group).sum(axis=1)
        low, high = first // group, last // group
        counts += [jnp.take(node_sizes, low), jnp.take(node_sizes, high)]
        index.append(jnp.where(unit_leaf // group == low, 2 * level, 2 * level + 1))
    nodes = [wanted]
    for which in range(1, reach[0] - 1):
        nodes.append(packed[which][None])
        inner = jnp.minimum(first + which, leaves - 1)
        counts.append(jnp.take(sizes, inner))
    total = jnp.stack(counts).astype(jnp.float32)
    grams = jnp.concatenate(nodes, axis=0) / total[:, None, None]
    small_eye = jnp.eye(fourth, dtype=jnp.float32)
    none = jnp.zeros_like(small_eye)
    eye = jnp.concatenate(
        [
            jnp.concatenate([small_eye, none], axis=1),
            jnp.concatenate([small_eye, small_eye], axis=1),
            jnp.concatenate([small_eye, none], axis=1),
            jnp.zeros((half, half), jnp.float32),
        ],
        axis=0,
    )
    inner_used = first + jnp.arange(1, reach[0] - 1, dtype=jnp.int32) < last
    used = jnp.concatenate([jnp.ones(len(slots), bool), inner_used])
    grams = jnp.where(used[:, None, None], grams, eye)
    inside = (unit_leaf > first) & (unit_leaf < last)
    index[0] = jnp.where(inside, len(slots) - 1 + unit_leaf - first, index[0])
    return make_bases(jnp.concatenate(index), grams, tree_rows, levels)


def shards(kernel, random_cols, tree_perm, leaf_units):
    rows_dev = kernel.shape[0] // lax.axis_size("col")
    incoming = sketch(kernel, random_cols, send_order(tree_perm, rows_dev))
    return bases_of(in_tree_order(incoming, tree_perm), tree_perm, leaf_units)


def solution(mesh):
    return jax.shard_map(
        shards,
        mesh=mesh,
        in_specs=(P("row", "col"), P("row", None), P(), P()),
        out_specs=P(None, ("row", "col"), None),
        check_vma=False,
    )
```

```python
import functools

import jax
import jax.numpy as jnp
from jax import lax
from jax.experimental import pallas as pl
from jax.experimental.pallas import tpu as pltpu
from jax.sharding import PartitionSpec as P

UNIT = 128
MINU = 4
MOSTU = 8
LEVELS = 3
BLOCK = 64
HIGHEST = lax.Precision.HIGHEST


def basis_kernel(index_ref, gram_ref, rows_ref, out_ref, work, block, high, low):
    nodes, _, half = gram_ref.shape
    width, fourth = 2 * half, half // 2
    count = width // BLOCK
    eye = (
        lax.broadcasted_iota(jnp.int32, (width, width), 0)
        == lax.broadcasted_iota(jnp.int32, (width, width), 1)
    ).astype(jnp.float32)

    @pl.loop(0, nodes)
    def _(node):
        corners = gram_ref[node, fourth:half, :]
        work[node, :half, :half] = gram_ref[node, :half, :]
        work[node, :half, half:width] = gram_ref[node, width - fourth :, :]
        work[node, half:, :half] = jnp.zeros((half, half), jnp.float32)
        work[node, half : width - fourth, half:width] = gram_ref[node, half : width - fourth, :]
        swapped = [corners[:, fourth:], corners[:, :fourth]]
        work[node, width - fourth :, half:width] = jnp.concatenate(swapped, axis=1)
        work[node, :, width:] = eye

    small = (
        lax.broadcasted_iota(jnp.int32, (nodes, BLOCK, BLOCK), 1)
        == lax.broadcasted_iota(jnp.int32, (nodes, BLOCK, BLOCK), 2)
    )

    @pl.loop(0, count)
    def _(step):
        for which in range(count):

            @pl.when(step == which)
            def _():
                start = which * BLOCK
                block[:, :, :BLOCK] = work[:, start : start + BLOCK, start : start + BLOCK]
                block[:, :, BLOCK:] = small.astype(jnp.float32)

        for column in range(BLOCK - 1):
            base = column // 8 * 8
            rest = block[:, base:, :]
            pivot_row = rest[:, column - base : column - base + 1, :]
            scale = 1.0 / pivot_row[:, :, column : column + 1]
            below = (
                lax.broadcasted_iota(jnp.int32, (nodes, BLOCK - base, 1), 1) > column - base
            )
            factor = jnp.where(below, rest[:, :, column : column + 1], 0.0)
            block[:, base:, :] = rest - factor * (pivot_row * scale)
        pivots = jnp.sum(jnp.where(small, block[:, :, :BLOCK], 0.0), axis=2, keepdims=True)
        block[:, :, BLOCK:] = block[:, :, BLOCK:] * lax.rsqrt(pivots)

        for which in range(count):

            @pl.when(step == which)
            def _():
                start = which * BLOCK
                after = start + BLOCK
                left = start // 128 * 128
                right = width + (after + 127) // 128 * 128

                @pl.loop(0, nodes, unroll=True)
                def _(node):
                    inverse = block[node][:, BLOCK:]
                    solved = jnp.dot(
                        inverse,
                        work[node, start:after, left:right],
                        preferred_element_type=jnp.float32,
                        precision=HIGHEST,
                    )
                    work[node, start:after, left:right] = solved
                    if after < width:
                        panel = solved[:, : width - left].T
                        change = jnp.dot(
                            panel[after - left :, :],
                            solved,
                            preferred_element_type=jnp.float32,
                            precision=HIGHEST,
                        )
                        work[node, after:, left:right] = work[node, after:, left:right] - change

    @pl.loop(0, nodes, unroll=True)
    def _(node):
        full = work[node, :, width:]
        top = full.astype(jnp.bfloat16)
        high[node] = top
        low[node] = (full - top.astype(jnp.float32)).astype(jnp.bfloat16)

    levels, rows, _ = out_ref.shape
    units = rows // UNIT

    @pl.loop(0, levels, unroll=True)
    def _(level):
        @pl.loop(0, units, unroll=True)
        def _(unit):
            node = index_ref[level * units + unit]
            where = pl.ds(pl.multiple_of(unit * UNIT, UNIT), UNIT)
            values = rows_ref[where, :]
            contract = (((1,), (1,)), ((), ()))
            total = lax.dot_general(
                values, low[node], contract, preferred_element_type=jnp.float32
            ) + lax.dot_general(values, high[node], contract, preferred_element_type=jnp.float32)
            out_ref[level, where, :] = total.astype(jnp.bfloat16)


def make_bases(index, grams, rows, levels):
    nodes, width = grams.shape[0], rows.shape[1]
    return pl.pallas_call(
        basis_kernel,
        out_shape=jax.ShapeDtypeStruct((levels, rows.shape[0], width), jnp.bfloat16),
        in_specs=[
            pl.BlockSpec(memory_space=pltpu.SMEM),
            pl.BlockSpec(memory_space=pltpu.VMEM),
            pl.BlockSpec(memory_space=pltpu.VMEM),
        ],
        out_specs=pl.BlockSpec(memory_space=pltpu.VMEM),
        scratch_shapes=[
            pltpu.VMEM((nodes, width, 2 * width), jnp.float32),
            pltpu.VMEM((nodes, BLOCK, 2 * BLOCK), jnp.float32),
            pltpu.VMEM((nodes, width, width), jnp.bfloat16),
            pltpu.VMEM((nodes, width, width), jnp.bfloat16),
        ],
        compiler_params=pltpu.CompilerParams(vmem_limit_bytes=40 * 2**20),
    )(index, grams, rows)


def running_sum(values):
    length = values.shape[-1]
    before = jnp.arange(length)[:, None] <= jnp.arange(length)[None, :]
    return jnp.sum(jnp.where(before, values[..., :, None], 0), axis=-2)


def running_count(flags):
    count, length = flags.shape
    pieces = length // 128
    before = jnp.arange(128)[:, None] <= jnp.arange(128)[None, :]
    within = jnp.dot(
        flags.reshape(-1, 128).astype(jnp.bfloat16),
        before.astype(jnp.bfloat16),
        preferred_element_type=jnp.float32,
    ).reshape(count, pieces, 128)
    total = within[:, :, 127]
    earlier = running_sum(total) - total
    return (within + earlier[:, :, None]).reshape(count, length).astype(jnp.int32)


MESH = pl.DeviceIdType.MESH
SLOTS = 2


def each(count, body):
    def step(index, carry):
        body(index)
        return carry

    lax.fori_loop(0, count, step, 0)


def sketch_kernel(
    sizes,
    k_ref,
    r_ref,
    order_ref,
    out_ref,
    wide,
    tall,
    rt,
    wt,
    w,
    acc,
    own,
    core_out,
    core_in,
    x_out,
    x_in,
    orders,
    product,
    pick,
    y_out,
    y_in,
    z_sum,
    z_out,
    z_own,
    z_in,
    r_out,
    r_in,
    wide_sem,
    tall_sem,
    order_sems,
    core_sems,
    x_sems,
    back_sems,
    y_sems,
    z_sems,
    r_sems,
):
    rows, cols, ys, cap, spread = sizes
    zs = cols // ys
    row, col = lax.axis_index("row"), lax.axis_index("col")
    z, y = lax.div(col, ys), lax.rem(col, ys)
    chunks, width, chunk = wt.shape
    half = width // 2
    blocks, rows_dev, _ = y_out.shape
    part = tall.shape[1]
    subs = rows_dev // part
    core = lax.rem(row, 2)
    pair = row + 1 - 2 * core
    xs = rows // 2
    mine = pl.ds(pl.multiple_of(core * half, half), half)
    other = pl.ds(pl.multiple_of(half - core * half, half), half)

    def wide_copy(step):
        slot = lax.rem(step, SLOTS)
        where = pl.ds(pl.multiple_of(step * chunk, chunk), chunk)
        return pltpu.make_async_copy(k_ref.at[:, where], wide.at[slot], wide_sem.at[slot])

    def tall_copy(step):
        slot = lax.rem(step, SLOTS)
        where = pl.ds(pl.multiple_of(step * part, part), part)
        return pltpu.make_async_copy(k_ref.at[where, :], tall.at[slot], tall_sem.at[slot])

    def send(source, target, sems, index, device):
        return pltpu.make_async_remote_copy(
            src_ref=source,
            dst_ref=target,
            send_sem=sems.at[(0, *index)],
            recv_sem=sems.at[(1, *index)],
            device_id=device,
            device_id_type=MESH,
        )

    def order_copy(away):
        device = (row, lax.rem(col + away, cols))
        return send(order_ref, orders.at[col], order_sems, (away - 1,), device)

    def core_copy(step):
        return send(core_out.at[step], core_in.at[step], core_sems, (step,), (pair, col))

    def x_copy(step, away):
        device = (lax.rem(row + 2 * away, rows), col)
        return send(x_out.at[step], x_in.at[away - 1, step], x_sems, (away - 1, step), device)

    def back_copy(step):
        where = wt.at[step, mine, :]
        return send(where, where, back_sems, (step,), (pair, col))

    y_rows, z_rows = rows_dev // ys, rows_dev // cols

    def y_copy(step, away):
        target = lax.rem(y + away, ys)
        where = pl.ds(pl.multiple_of(target * y_rows, y_rows), y_rows)
        device = (row, z * ys + target)
        return send(
            y_out.at[step, where, :], y_in.at[away - 1, step], y_sems, (away - 1, step), device
        )

    def z_copy(step, away):
        target = lax.rem(z + away, zs)
        where = pl.ds(pl.multiple_of(target * z_rows, z_rows), z_rows)
        device = (row, target * ys + y)
        return send(
            z_out.at[step, where, :], z_in.at[away - 1, step], z_sems, (away - 1, step), device
        )

    def r_copy(step, away):
        target = lax.rem(row + away, rows)
        where = pl.ds(pl.multiple_of(target * cap, cap), cap)
        return send(
            r_out.at[step, where, :],
            r_in.at[row, step],
            r_sems,
            (away - 1, step),
            (target, col),
        )

    for step in range(SLOTS):
        wide_copy(step).start()

    barrier = pltpu.get_barrier_semaphore()
    for away in range(1, rows):
        device = (lax.rem(row + away, rows), col)
        pl.semaphore_signal(barrier, inc=1, device_id=device, device_id_type=MESH)
    for away in range(1, cols):
        device = (row, lax.rem(col + away, cols))
        pl.semaphore_signal(barrier, inc=1, device_id=device, device_id_type=MESH)

    def turn(step):
        where = pl.ds(pl.multiple_of(step * 512, 512), 512)
        rt[:, where] = r_ref[where, :].T

    each(r_ref.shape[0] // 512, turn)
    pl.semaphore_wait(barrier, rows + cols - 2)
    for away in range(1, cols):
        order_copy(away).start()
    orders[col] = order_ref[...]

    def first(step):
        @pl.when(step < chunks)
        def _():
            wide_copy(step).wait()
            acc[...] = jnp.dot(
                rt[...], wide[lax.rem(step, SLOTS)], preferred_element_type=jnp.float32
            )

            @pl.when(step + SLOTS < chunks)
            def _():
                wide_copy(step + SLOTS).start()

            core_out[step] = acc[other, :].astype(jnp.bfloat16)
            own[step] = acc[mine, :]
            core_copy(step).start()

        @pl.when(step == chunks - 1)
        def _():
            for ahead in range(SLOTS):
                tall_copy(ahead).start()

        @pl.when((step >= 1) & (step <= chunks))
        def _():
            here = step - 1
            core_copy(here).wait()
            total = own[here] + core_in[here].astype(jnp.float32)
            own[here] = total
            x_out[here] = total.astype(jnp.bfloat16)
            for away in range(1, xs):
                x_copy(here, away).start()

        @pl.when((step >= 3) & (step <= chunks + 2))
        def _():
            here = step - 3
            total = own[here]
            for away in range(1, xs):
                x_copy(here, away).wait()
                total = total + x_in[away - 1, here].astype(jnp.float32)
            wt[here, mine, :] = total.astype(jnp.bfloat16)
            back_copy(here).start()

        @pl.when(step >= 4)
        def _():
            here = step - 4
            back_copy(here).wait()
            w[pl.ds(pl.multiple_of(here * chunk, chunk), chunk), :] = wt[here].T

    each(chunks + 4, first)
    for away in range(1, cols):
        order_copy(away).wait()

    lane = lax.broadcasted_iota(jnp.int32, (128, 128), 1).astype(jnp.float32)

    def second(step):
        @pl.when(step < blocks)
        def _():
            for sub in range(subs):
                index = step * subs + sub
                tall_copy(index).wait()
                product[sub * part : (sub + 1) * part, :] = jnp.dot(
                    tall[lax.rem(index, SLOTS)], w[...], preferred_element_type=jnp.float32
                ).astype(jnp.bfloat16)

                @pl.when(index + SLOTS < blocks * subs)
                def _():
                    tall_copy(index + SLOTS).start()

            for piece in range(rows_dev // 128):
                wanted = jnp.broadcast_to(orders[step, piece : piece + 1, :], (128, 128)).T
                for tile in range(rows_dev // 128):
                    hit = jnp.where(wanted == lane + 128.0 * tile, 1.0, 0.0)
                    pick[piece * 128 : (piece + 1) * 128, tile * 128 : (tile + 1) * 128] = (
                        hit.astype(jnp.bfloat16)
                    )
            y_out[step] = jnp.dot(
                pick[...], product[...], preferred_element_type=jnp.float32
            ).astype(jnp.bfloat16)
            for away in range(1, ys):
                y_copy(step, away).start()

        @pl.when((step >= 1) & (step <= blocks))
        def _():
            here = step - 1
            kept = pl.ds(pl.multiple_of(y * y_rows, y_rows), y_rows)
            total = y_out[here, kept, :].astype(jnp.float32)
            for away in range(1, ys):
                y_copy(here, away).wait()
                total = total + y_in[away - 1, here].astype(jnp.float32)
            z_sum[...] = total
            z_out[here] = total.astype(jnp.bfloat16)
            z_own[here] = z_sum[pl.ds(pl.multiple_of(z * z_rows, z_rows), z_rows), :]
            for away in range(1, zs):
                z_copy(here, away).start()

        @pl.when(step >= 3)
        def _():
            here = step - 3
            total = z_own[here]
            for away in range(1, zs):
                z_copy(here, away).wait()
                total = total + z_in[away - 1, here].astype(jnp.float32)
            if not spread:
                out_ref[here] = total.astype(jnp.bfloat16)
            else:
                r_out[here] = total.astype(jnp.bfloat16)
                for away in range(1, rows):
                    r_copy(here, away).start()

    each(blocks + 3, second)
    if spread:
        kept = pl.ds(pl.multiple_of(row * cap, cap), cap)
        r_in[row] = r_out[:, kept, :]

        def last(step):
            for away in range(1, rows):
                r_copy(step, away).wait()

        each(blocks, last)
        out_ref[...] = r_in[...]


def sketch(kernel, random_cols, order):
    height, length = kernel.shape
    width = random_cols.shape[1]
    rows, cols = lax.axis_size("row"), lax.axis_size("col")
    rows_dev = height // cols
    ys = max(cols // 4, 1)
    zs = cols // ys
    cap = rows_dev // (rows * cols)
    spread = cap % 16 == 0
    chunk = min(512, length)
    chunks = length // chunk
    part = min(512, rows_dev)
    half = width // 2
    y_rows, z_rows = rows_dev // ys, rows_dev // cols
    bf, f32 = jnp.bfloat16, jnp.float32
    shape = (rows, cols, cap, width) if spread else (cols, z_rows, width)
    peers = max(rows // 2 - 1, 1)
    dma = pltpu.SemaphoreType.DMA
    got = pl.pallas_call(
        functools.partial(sketch_kernel, (rows, cols, ys, cap, spread)),
        out_shape=jax.ShapeDtypeStruct(shape, bf),
        in_specs=[
            pl.BlockSpec(memory_space=pl.ANY),
            pl.BlockSpec(memory_space=pltpu.VMEM),
            pl.BlockSpec(memory_space=pltpu.VMEM),
        ],
        out_specs=pl.BlockSpec(memory_space=pltpu.VMEM),
        scratch_shapes=[
            pltpu.VMEM((SLOTS, height, chunk), bf),
            pltpu.VMEM((SLOTS, part, length), bf),
            pltpu.VMEM((width, height), bf),
            pltpu.VMEM((chunks, width, chunk), bf),
            pltpu.VMEM((length, width), bf),
            pltpu.VMEM((width, chunk), f32),
            pltpu.VMEM((chunks, half, chunk), f32),
            pltpu.VMEM((chunks, half, chunk), bf),
            pltpu.VMEM((chunks, half, chunk), bf),
            pltpu.VMEM((chunks, half, chunk), bf),
            pltpu.VMEM((peers, chunks, half, chunk), bf),
            pltpu.VMEM((cols, *order.shape), f32),
            pltpu.VMEM((rows_dev, width), bf),
            pltpu.VMEM((rows_dev, rows_dev), bf),
            pltpu.VMEM((cols, rows_dev, width), bf),
            pltpu.VMEM((max(ys - 1, 1), cols, y_rows, width), bf),
            pltpu.VMEM((y_rows, width), f32),
            pltpu.VMEM((cols, y_rows, width), bf),
            pltpu.VMEM((cols, z_rows, width), f32),
            pltpu.VMEM((zs - 1, cols, z_rows, width), bf),
            pltpu.VMEM((cols, z_rows, width), bf),
            pltpu.VMEM((rows, cols, cap if spread else 16, width), bf),
            dma((SLOTS,)),
            dma((SLOTS,)),
            dma((2, cols - 1)),
            dma((2, chunks)),
            dma((2, peers, chunks)),
            dma((2, chunks)),
            dma((2, max(ys - 1, 1), cols)),
            dma((2, zs - 1, cols)),
            dma((2, rows - 1, cols)),
        ],
        compiler_params=pltpu.CompilerParams(
            collective_id=0, has_side_effects=True, vmem_limit_bytes=60 * 2**20
        ),
        cost_estimate=pl.CostEstimate(
            flops=4 * height * length * width,
            bytes_accessed=4 * height * length,
            transcendentals=0,
        ),
    )(kernel, random_cols, order)
    if spread:
        return got.reshape(rows_dev, width)
    got = got.reshape(cols, rows, cap, width).swapaxes(0, 1).reshape(rows_dev, width)
    return lax.all_to_all(got, "row", split_axis=0, concat_axis=0, tiled=True)


def send_order(tree_perm, rows_dev):
    rows, cols = lax.axis_size("row"), lax.axis_size("col")
    ys = max(cols // 4, 1)
    devices = rows * cols
    device = lax.axis_index(("row", "col"))
    capacity = rows_dev // devices
    grid = tree_perm.reshape(devices, rows_dev)
    mine = grid // rows_dev == device
    rank = running_count(mine) - 1
    slots = jnp.arange(capacity, dtype=jnp.int32)
    chosen = mine[:, None, :] & (rank[:, None, :] == slots[None, :, None])
    order = jnp.sum(jnp.where(chosen, (grid % rows_dev)[:, None, :], 0), axis=2)
    order = order.reshape(rows, cols // ys, ys, capacity).transpose(2, 1, 0, 3)
    order = order.reshape(rows_dev // 128, 128).astype(jnp.float32)
    return jnp.pad(order, ((0, -order.shape[0] % 8), (0, 0)))


def in_tree_order(incoming, tree_perm):
    rows_dev = incoming.shape[0]
    devices = tree_perm.shape[0] // rows_dev
    device = lax.axis_index(("row", "col"))
    capacity = rows_dev // devices
    wanted = lax.dynamic_slice_in_dim(tree_perm, device * rows_dev, rows_dev)
    source = wanted // rows_dev
    order = jnp.arange(rows_dev, dtype=jnp.int32)
    ahead = (source[None, :] == source[:, None]) & (order[None, :] < order[:, None])
    pick = source * capacity + jnp.sum(ahead, axis=1)
    return jnp.take(incoming, pick, axis=0, mode="clip")


def bases_of(tree_rows, tree_perm, leaf_units):
    rows_dev, width = tree_rows.shape
    devices = tree_perm.shape[0] // rows_dev
    device = lax.axis_index(("row", "col"))
    sizes = UNIT * (MINU - 1 + leaf_units)
    leaves = sizes.shape[0]
    ends = running_sum(sizes)
    levels = LEVELS + 1
    units = rows_dev // UNIT
    starts = jnp.arange(devices, dtype=jnp.int32) * rows_dev
    first_leaf = jnp.sum(starts[:, None] >= ends[None, :], axis=1)
    last_leaf = jnp.sum((starts + rows_dev - 1)[:, None] >= ends[None, :], axis=1)
    unit_start = device * rows_dev + jnp.arange(units, dtype=jnp.int32) * UNIT
    unit_leaf = jnp.sum(unit_start[:, None] >= ends[None, :], axis=1)

    reach = [2 + max(rows_dev - 2 * UNIT, 0) // (UNIT * MINU * 2**t) for t in range(levels)]
    half, fourth = width // 2, width // 4
    lanes = half if (width + fourth) % devices == 0 else fourth
    slots = [(level, which) for level in range(levels) for which in range(2)]
    first = jnp.take(first_leaf, device)
    touched = first + jnp.arange(reach[0], dtype=jnp.int32)
    unit_mask = (unit_leaf[None, :] == touched[:, None]).astype(jnp.bfloat16)
    mask = jnp.repeat(unit_mask, UNIT, axis=1)
    packed = []
    for which in range(reach[0]):
        full = lax.dot_general(
            tree_rows * mask[which][:, None],
            tree_rows,
            (((0,), (0,)), ((), ())),
            preferred_element_type=jnp.float32,
        )
        corners = [full[-fourth:, -fourth:], full[fourth:half, fourth:half]]
        part = jnp.concatenate(
            [
                full[:fourth, :half],
                jnp.concatenate(corners, axis=1),
                full[half:-fourth, half:],
                full[:half, half:],
            ],
            axis=0,
        )
        packed.append(part)
    outgoing = jnp.concatenate([part.reshape(devices, -1, lanes) for part in packed], axis=1)
    incoming = lax.all_to_all(outgoing, ("row", "col"), split_axis=0, concat_axis=0, tiled=True)
    incoming = incoming.reshape(devices * reach[0], -1)
    part_leaf = (first_leaf[:, None] + jnp.arange(reach[0], dtype=jnp.int32)).reshape(-1)
    chosen = jnp.stack(
        [
            part_leaf[None, :] // 2**level == ((first_leaf, last_leaf)[which] // 2**level)[:, None]
            for level, which in slots
        ],
        axis=1,
    )
    sums = jnp.dot(
        chosen.astype(jnp.float32).reshape(devices * len(slots), -1),
        incoming,
        preferred_element_type=jnp.float32,
        precision=HIGHEST,
    )
    sums = sums.reshape(devices, -1, lanes)
    wanted = lax.all_to_all(sums, ("row", "col"), split_axis=0, concat_axis=0, tiled=True)
    wanted = wanted.reshape(devices, len(slots), -1, lanes).swapaxes(0, 1)
    wanted = wanted.reshape(len(slots), width + fourth, half)

    last = jnp.take(last_leaf, device)
    counts, index = [], []
    for level in range(levels):
        group = 2**level
        node_sizes = sizes.reshape(leaves // group, group).sum(axis=1)
        low, high = first // group, last // group
        counts += [jnp.take(node_sizes, low), jnp.take(node_sizes, high)]
        index.append(jnp.where(unit_leaf // group == low, 2 * level, 2 * level + 1))
    nodes = [wanted]
    for which in range(1, reach[0] - 1):
        nodes.append(packed[which][None])
        inner = jnp.minimum(first + which, leaves - 1)
        counts.append(jnp.take(sizes, inner))
    total = jnp.stack(counts).astype(jnp.float32)
    grams = jnp.concatenate(nodes, axis=0) / total[:, None, None]
    small_eye = jnp.eye(fourth, dtype=jnp.float32)
    none = jnp.zeros_like(small_eye)
    eye = jnp.concatenate(
        [
            jnp.concatenate([small_eye, none], axis=1),
            jnp.concatenate([small_eye, small_eye], axis=1),
            jnp.concatenate([small_eye, none], axis=1),
            jnp.zeros((half, half), jnp.float32),
        ],
        axis=0,
    )
    inner_used = first + jnp.arange(1, reach[0] - 1, dtype=jnp.int32) < last
    used = jnp.concatenate([jnp.ones(len(slots), bool), inner_used])
    grams = jnp.where(used[:, None, None], grams, eye)
    inside = (unit_leaf > first) & (unit_leaf < last)
    index[0] = jnp.where(inside, len(slots) - 1 + unit_leaf - first, index[0])
    return make_bases(jnp.concatenate(index), grams, tree_rows, levels)


def shards(kernel, random_cols, tree_perm, leaf_units):
    rows_dev = kernel.shape[0] // lax.axis_size("col")
    incoming = sketch(kernel, random_cols, send_order(tree_perm, rows_dev))
    return bases_of(in_tree_order(incoming, tree_perm), tree_perm, leaf_units)


def solution(mesh):
    return jax.shard_map(
        shards,
        mesh=mesh,
        in_specs=(P("row", "col"), P("row", None), P(), P()),
        out_specs=P(None, ("row", "col"), None),
        check_vma=False,
    )
```
